32 devices in a mesh: dp: 8 (over z, x), fsdp: 4 (over y, core).
Axes of the slice: x: 2, y: 2, z: 4, core: 2. Of those that a mesh axis runs over, the one named last changes fastest.
Arguments:
- cell_tokens: bfloat16 [2, 32, 256, 768], P(None, ('dp', 'fsdp')), may hold values from -6 to 6
- lengths: int32 [2, 32], P(None, ('dp', 'fsdp')), may hold values from 85 to 256, as said below
- gene_ids: int32 [2, 32, 256], P(None, ('dp', 'fsdp')), may hold values from 0 to 19263, as said below
- grad_gene: bfloat16 [2, 32, 256, 768], P(None, ('dp', 'fsdp')), may hold values from -6 to 6
- ln1_gain: bfloat16 [768], P(('dp', 'fsdp')), may hold values from 0.5 to 1.5
- ln1_bias: bfloat16 [768], P(('dp', 'fsdp')), may hold values from -1 to 1
- w_qkv: bfloat16 [768, 2304], P(('dp', 'fsdp')), may hold values from -0.3125 to 0.3125
- q_bias: bfloat16 [768], P(('dp', 'fsdp')), may hold values from -1 to 1
- v_bias: bfloat16 [768], P(('dp', 'fsdp')), may hold values from -1 to 1
- w_out: bfloat16 [768, 768], P(('dp', 'fsdp')), may hold values from -1.75 to 1.75
- out_bias: bfloat16 [768], P(('dp', 'fsdp')), may hold values from -1 to 1
- ln2_gain: bfloat16 [768], P(('dp', 'fsdp')), may hold values from 0.5 to 1.5
- ln2_bias: bfloat16 [768], P(('dp', 'fsdp')), may hold values from -1 to 1
- w_up: bfloat16 [768, 3072], P(('dp', 'fsdp')), may hold values from -0.21875 to 0.21875
- up_bias: bfloat16 [3072], P(('dp', 'fsdp')), may hold values from -1 to 1
- w_down: bfloat16 [3072, 768], P(('dp', 'fsdp')), may hold values from -0.109375 to 0.109375
- down_bias: bfloat16 [768], P(('dp', 'fsdp')), may hold values from -1 to 1
Outputs:
- gene_rows: bfloat16 [2, 32, 256, 768], P(None, ('dp', 'fsdp'))
- grad_tokens: float32 [2, 32, 256, 768], P(None, ('dp', 'fsdp'))
- grad_ln1_gain: float32 [768], P(('dp', 'fsdp'))
- grad_ln1_bias: float32 [768], P(('dp', 'fsdp'))
- grad_w_qkv: float32 [768, 2304], P(('dp', 'fsdp'))
- grad_q_bias: float32 [768], P(('dp', 'fsdp'))
- grad_v_bias: float32 [768], P(('dp', 'fsdp'))
- grad_w_out: float32 [768, 768], P(('dp', 'fsdp'))
- grad_out_bias: float32 [768], P(('dp', 'fsdp'))
- grad_ln2_gain: float32 [768], P(('dp', 'fsdp'))
- grad_ln2_bias: float32 [768], P(('dp', 'fsdp'))
- grad_w_up: float32 [768, 3072], P(('dp', 'fsdp'))
- grad_up_bias: float32 [3072], P(('dp', 'fsdp'))
- grad_w_down: float32 [3072, 768], P(('dp', 'fsdp'))
- grad_down_bias: float32 [768], P(('dp', 'fsdp'))
The draws below stay inside these ranges and needn't reach their ends.
Inputs may be any that keep to these rules, and one draw needn't show every extreme that they name: `lengths`: in every micro-batch some cell has exactly 256 valid slots. `gene_ids`: in every cell each owner (gene // 2408) occurs in exactly 32 of the 256 slots, so the valid slots of a cell hold at most 32 tokens of one owner, and a full cell exactly 32 of each.
All inputs are finite; a program needn't handle non-finite values.
Results may differ from the reference program's by a relative error of at most 0.013.
Values may be sent and summed in bfloat16 or wider, within the bound.
No kernel may reach another device: no remote copies, remote signals or barrier semaphores. Data moves between devices by JAX's collectives and lax.ppermute only.
A program may use at most 192 MiB of HBM per device.

```python
import jax
import jax.numpy as jnp
from jax import lax

D = 768
HD = 64
FF = 3072
MB = 2
LEN = 256
CELLS = 32
CAP = 32
GENE_SPAN = 2408
N_DP = 8
N_FSDP = 4
DEVICES = 32


def draw_lengths(key, part):
    extent = LEN - LEN // 3
    key_one, key_two, key_three = jax.random.split(key, 3)
    first = jax.random.randint(key_one, (MB, CELLS), 0, extent + 1)
    second = jax.random.randint(key_two, (MB, CELLS), 0, extent + 1)
    drawn = LEN // 3 + first * second // extent
    longest = jax.random.randint(key_three, (MB, 1), 0, CELLS)
    chosen = jnp.arange(CELLS)[None, :] == longest
    return jnp.where(chosen, LEN, drawn).astype(jnp.int32)


def draw_gene_ids(key, part):
    key_one, key_two = jax.random.split(key, 2)
    key_list = jax.random.split(key_one, MB * CELLS)
    orders = jax.vmap(lambda single: jax.random.permutation(single, LEN))(key_list)
    owner_index = (orders.reshape(MB, CELLS, LEN) % (LEN // CAP)).astype(jnp.int32)
    offset = jax.random.randint(key_two, (MB, CELLS, LEN), 0, GENE_SPAN)
    return (owner_index * GENE_SPAN + offset).astype(jnp.int32)


def block_scale(key, shape, shards, least, high):
    factor_of, own = 1.0, jax.random.fold_in(key, 6)
    for axis_at, parts in shards:
        heights = jnp.exp(jax.random.uniform(jax.random.fold_in(own, axis_at), (parts,), jnp.float32, least / len(shards), high / len(shards)))
        factor_of = factor_of * jnp.repeat(heights, shape[axis_at] // parts).reshape([-1 if axis == axis_at else 1 for axis in range(len(shape))])
    return factor_of


def scatter_about(key, shape, scale, limit, shards=(), kind=jnp.bfloat16):
    factor_of = block_scale(key, shape, shards, -0.22, 0.18) if shards else 1.0
    array = jax.random.normal(key, shape, jnp.float32) * scale * factor_of
    return jnp.minimum(jnp.maximum(array, -limit), limit).astype(kind)


def setup_inputs(seed: int = 0) -> dict:
    streams_of = jax.random.split(jax.random.key(seed), 18)
    return {
        "cell_tokens": scatter_about(streams_of[0], (MB, CELLS, LEN, D), 1.0, 6.0, ((1, 32),)),
        "lengths": draw_lengths(jax.random.fold_in(streams_of[17], 71), 0),
        "gene_ids": draw_gene_ids(jax.random.fold_in(streams_of[17], 71), 0),
        "grad_gene": scatter_about(streams_of[3], (MB, DEVICES, N_DP * CAP, D), 1.0, 6.0, ((1, 32),)),
        "ln1_gain": jnp.clip(1.0 + 0.1 * jax.random.normal(streams_of[4], (D,), jnp.float32), 0.5, 1.5).astype(jnp.bfloat16),
        "ln1_bias": scatter_about(streams_of[5], (D,), 0.2, 1.0, ((0, 32),)),
        "w_qkv": scatter_about(streams_of[6], (D, 3 * D), (D // 2) ** -0.5, 0.3125, ((0, 32),)),
        "q_bias": scatter_about(streams_of[7], (D,), 0.2, 1.0, ((0, 32),)),
        "v_bias": scatter_about(streams_of[8], (D,), 0.2, 1.0, ((0, 32),)),
        "w_out": scatter_about(streams_of[9], (D, D), (D // 64) ** -0.5, 1.75, ((0, 32),)),
        "out_bias": scatter_about(streams_of[10], (D,), 0.2, 1.0, ((0, 32),)),
        "ln2_gain": jnp.clip(1.0 + 0.1 * jax.random.normal(streams_of[11], (D,), jnp.float32), 0.5, 1.5).astype(jnp.bfloat16),
        "ln2_bias": scatter_about(streams_of[12], (D,), 0.2, 1.0, ((0, 32),)),
        "w_up": scatter_about(streams_of[13], (D, FF), D ** -0.5, 0.21875, ((0, 32),)),
        "up_bias": scatter_about(streams_of[14], (FF,), 0.2, 1.0, ((0, 32),)),
        "w_down": scatter_about(streams_of[15], (FF, D), FF ** -0.5, 0.109375, ((0, 32),)),
        "down_bias": scatter_about(streams_of[16], (D,), 0.2, 1.0, ((0, 32),)),
    }


@jax.custom_vjp
def low(v):
    return lax.optimization_barrier(v.astype(jnp.bfloat16)).astype(jnp.float32)

@jax.custom_vjp
def low_back(v):
    return v

def low_keep(v):
    return (low(v), None)

def low_pass(kept, grad):
    return (grad,)

def back_keep(v):
    return (v, None)

def back_low(kept, grad):
    return (low(grad),)
low.defvjp(low_keep, low_pass)
low_back.defvjp(back_keep, back_low)

def layer_norm(values, norm_gain, norm_shift):
    center = values - lax.optimization_barrier(jnp.mean(values, axis=-1, keepdims=True))
    spread = lax.optimization_barrier(jnp.mean(center * center, axis=-1, keepdims=True))
    return center * lax.rsqrt(spread + 1e-05) * norm_gain + norm_shift

def attend_cell(bundle):
    queries, keys_low, values, valid_mask = bundle
    scores = jnp.einsum('qhd,khd->hqk', queries, keys_low, precision=lax.Precision.HIGHEST) * 0.125
    scores = low_back(scores)
    scores = jnp.where(valid_mask[None, None, :], scores, -1e+30)
    probability = low(jax.nn.softmax(scores, axis=-1))
    return jnp.einsum('hqk,khd->qhd', probability, values, precision=lax.Precision.HIGHEST)

def project(left_side, right_side):
    return jnp.einsum('gtd,de->gte', left_side, right_side, precision=lax.Precision.HIGHEST)

def layer(params, tokens, valid_mask):
    gain_one, shift_one, w_qkv, q_bias, v_bias, w_out, out_bias, gain_two, shift_two, w_up, up_bias, w_down, down_bias = params
    group_size, length, model_width = tokens.shape
    shaped = (group_size, length, model_width // HD, HD)
    normed_one = low(layer_norm(tokens, gain_one, shift_one))
    projected = project(normed_one, w_qkv)
    queries = low_back(low(projected[..., :model_width] + q_bias)).reshape(shaped)
    keys_low = low_back(low(projected[..., model_width:2 * model_width])).reshape(shaped)
    values = low_back(low(projected[..., 2 * model_width:] + v_bias)).reshape(shaped)
    attended = lax.map(jax.checkpoint(attend_cell), (queries, keys_low, values, valid_mask))
    attended = low_back(low(attended.reshape(group_size, length, model_width)))
    branch_one = low_back(project(attended, w_out) + out_bias)
    residual = tokens + branch_one
    normed_two = low(layer_norm(residual, gain_two, shift_two))
    up_value = low_back(project(normed_two, w_up) + up_bias)
    hidden = low(jax.nn.gelu(up_value, approximate=False))
    branch_two = low_back(project(hidden, w_down) + down_bias)
    return residual + branch_two

def place_rows(buffer, targets, row_values):
    return buffer.at[targets].set(row_values)

def reference(cell_tokens, lengths, gene_ids, grad_gene, ln1_gain, ln1_bias, w_qkv, q_bias, v_bias, w_out, out_bias, ln2_gain, ln2_bias, w_up, up_bias, w_down, down_bias):
    params = tuple((weight.astype(jnp.float32) for weight in (ln1_gain, ln1_bias, w_qkv, q_bias, v_bias, w_out, out_bias, ln2_gain, ln2_bias, w_up, up_bias, w_down, down_bias)))
    group_size = max(1, 4096 // LEN)
    rounds = MB * CELLS // group_size
    slots_all = N_DP * CAP
    positions = jnp.arange(LEN).astype(jnp.int32)
    valid_mask = positions[None, None, :] < lengths[:, :, None]
    owner_index = (gene_ids // GENE_SPAN).astype(jnp.int32)
    owner_list = jnp.arange(N_DP).astype(jnp.int32)
    owner_hits = ((owner_index[..., None] == owner_list[None, None, None, :]) & valid_mask[..., None]).astype(jnp.int32)
    owner_rank = lax.optimization_barrier(jnp.sum(jnp.cumsum(owner_hits, axis=2) * owner_hits, axis=-1)) - 1
    slot_index = jnp.where(valid_mask, owner_index * CAP + owner_rank, slots_all).astype(jnp.int32)
    cells_back = grad_gene.reshape(MB, N_DP, N_FSDP, N_DP, CAP, D).transpose(0, 3, 2, 1, 4, 5)
    cells_back = cells_back.reshape(rounds, group_size, slots_all, D)
    cells_back = jnp.concatenate([cells_back, jnp.zeros((rounds, group_size, 1, D), jnp.bfloat16)], axis=2)
    token_groups = cell_tokens.reshape(rounds, group_size, LEN, D)
    valid_groups = valid_mask.reshape(rounds, group_size, LEN)
    slot_groups = slot_index.reshape(rounds, group_size, LEN)

    def one_round(totals, inputs):
        tokens, valid_group, slot_group, back_group = inputs
        cotangent = jnp.take_along_axis(back_group, slot_group[..., None], axis=1).astype(jnp.float32)

        def forward(weights, tokens_float):
            return layer(weights, tokens_float, valid_group)
        result, pullback = jax.vjp(forward, params, tokens.astype(jnp.float32))
        grad_weights, grad_inputs = pullback(cotangent)
        totals = jax.tree.map(jnp.add, totals, grad_weights)
        buffers = jnp.zeros((group_size, slots_all + 1, D), jnp.bfloat16)
        buffers = jax.vmap(place_rows)(buffers, slot_group, result.astype(jnp.bfloat16))
        return (totals, (buffers[:, :slots_all], grad_inputs))
    start = jax.tree.map(jnp.zeros_like, params)
    totals, (buffers, grad_inputs) = lax.scan(one_round, start, (token_groups, valid_groups, slot_groups, cells_back))
    gene_rows = buffers.reshape(MB, N_DP, N_FSDP, N_DP, CAP, D).transpose(0, 3, 2, 1, 4, 5)
    gene_rows = gene_rows.reshape(MB, DEVICES, slots_all, D)
    grad_tokens = grad_inputs.reshape(MB, CELLS, LEN, D)
    return (gene_rows, grad_tokens, totals[0], totals[1], totals[2], totals[3], totals[4], totals[5], totals[6], totals[7], totals[8], totals[9], totals[10], totals[11], totals[12])
```

```python
from functools import partial

import jax
import jax.numpy as jnp
from jax import lax
from jax.sharding import PartitionSpec as P

HD = 64
GENES = 19264


def layer_norm(values, norm_gain, norm_shift):
    center = values - jnp.mean(values, axis=-1, keepdims=True)
    spread = jnp.mean(center * center, axis=-1, keepdims=True)
    return center * lax.rsqrt(spread + 1e-05) * norm_gain + norm_shift


def contract_rows(left_side, right_side):
    return lax.dot_general(
        left_side, right_side, (((0,), (0,)), ((), ())), preferred_element_type=jnp.float32
    )


def contract_cols(left_side, right_side):
    return lax.dot_general(
        left_side, right_side, (((1,), (1,)), ((), ())), preferred_element_type=jnp.float32
    )


def masked_scores(query_block, keys_low, valid_mask):
    scores = (
        jnp.einsum("qhd,khd->hqk", query_block, keys_low, preferred_element_type=jnp.float32)
        * 0.125
    )
    return jnp.where(valid_mask[None, None, :], scores, -1e30)


def attend_forward(queries, keys_low, values, valid_mask):
    length, head_count, head_dim = queries.shape
    block_rows = min(length, 512)

    def one_block(query_block):
        scores = masked_scores(query_block, keys_low, valid_mask)
        highest = jnp.max(scores, axis=-1, keepdims=True)
        weights = jnp.exp(scores - highest)
        totals = jnp.sum(weights, axis=-1, keepdims=True)
        probability = (weights / totals).astype(jnp.bfloat16)
        attended = jnp.einsum(
            "hqk,khd->qhd", probability, values, preferred_element_type=jnp.float32
        )
        return (attended.astype(jnp.bfloat16), (highest + jnp.log(totals))[..., 0])

    attended, logsum = lax.map(
        one_block, queries.reshape(length // block_rows, block_rows, head_count, head_dim)
    )
    return (attended.reshape(length, head_count * head_dim), logsum)


def attend_backward(queries, keys_low, values, valid_mask, logsum, grad_attended):
    length, head_count, head_dim = queries.shape
    block_rows = min(length, 512)
    block_count = length // block_rows
    query_blocks = queries.reshape(block_count, block_rows, head_count, head_dim)
    grad_blocks = grad_attended.reshape(block_count, block_rows, head_count, head_dim)

    def one_block(carried, inputs):
        key_total, value_total = carried
        query_block, grad_block, block_logsum = inputs
        scores = masked_scores(query_block, keys_low, valid_mask)
        probability = jnp.exp(scores - block_logsum[..., None])
        grad_probability = jnp.einsum(
            "qhd,khd->hqk", grad_block, values, preferred_element_type=jnp.float32
        )
        row_inner = jnp.sum(probability * grad_probability, axis=-1, keepdims=True)
        grad_scores = (probability * (grad_probability - row_inner)).astype(jnp.bfloat16)
        grad_query = (
            jnp.einsum("hqk,khd->qhd", grad_scores, keys_low, preferred_element_type=jnp.float32)
            * 0.125
        )
        key_total = (
            key_total
            + jnp.einsum(
                "hqk,qhd->khd", grad_scores, query_block, preferred_element_type=jnp.float32
            )
            * 0.125
        )
        value_total = value_total + jnp.einsum(
            "hqk,qhd->khd",
            probability.astype(jnp.bfloat16),
            grad_block,
            preferred_element_type=jnp.float32,
        )
        return ((key_total, value_total), grad_query.astype(jnp.bfloat16))

    zero_grads = jnp.zeros((length, head_count, head_dim), jnp.float32)
    (key_total, value_total), grad_queries = lax.scan(
        one_block, (zero_grads, zero_grads), (query_blocks, grad_blocks, logsum)
    )
    model_width = head_count * head_dim
    return (
        grad_queries.reshape(length, model_width),
        key_total.astype(jnp.bfloat16).reshape(length, model_width),
        value_total.astype(jnp.bfloat16).reshape(length, model_width),
    )


def micro_step(weights, tokens, cell_length, genes_here, cotangent, owners, capacity, gene_span):
    (
        gain_one,
        shift_one,
        w_qkv,
        q_bias,
        v_bias,
        w_out,
        out_bias,
        gain_two,
        shift_two,
        w_up,
        up_bias,
        w_down,
        down_bias,
    ) = weights
    length, model_width = tokens.shape
    shaped = (length, model_width // HD, HD)
    valid_mask = jnp.arange(length) < cell_length
    owner_index = genes_here // gene_span
    owner_hits = (
        (owner_index[:, None] == jnp.arange(owners)[None, :]) & valid_mask[:, None]
    ).astype(jnp.int32)
    owner_rank = jnp.sum(jnp.cumsum(owner_hits, axis=0) * owner_hits, axis=1) - 1
    slot_index = jnp.where(valid_mask, owner_index * capacity + owner_rank, -1)
    select = (jnp.arange(owners * capacity)[:, None] == slot_index[None, :]).astype(jnp.bfloat16)
    tokens_float = tokens.astype(jnp.float32)
    gain_one_f = gain_one.astype(jnp.float32)
    shift_one_f = shift_one.astype(jnp.float32)
    gain_two_f = gain_two.astype(jnp.float32)
    shift_two_f = shift_two.astype(jnp.float32)
    normed_one = layer_norm(tokens_float, gain_one_f, shift_one_f).astype(jnp.bfloat16)
    projected = jnp.dot(normed_one, w_qkv, preferred_element_type=jnp.float32)
    queries = (projected[:, :model_width] + q_bias.astype(jnp.float32)).astype(jnp.bfloat16)
    keys_low = projected[:, model_width : 2 * model_width].astype(jnp.bfloat16)
    values = (projected[:, 2 * model_width :] + v_bias.astype(jnp.float32)).astype(jnp.bfloat16)
    attended, logsum = attend_forward(
        queries.reshape(shaped), keys_low.reshape(shaped), values.reshape(shaped), valid_mask
    )
    residual = (
        tokens_float
        + jnp.dot(attended, w_out, preferred_element_type=jnp.float32)
        + out_bias.astype(jnp.float32)
    )
    normed_two = layer_norm(residual, gain_two_f, shift_two_f).astype(jnp.bfloat16)
    up_value = jnp.dot(normed_two, w_up, preferred_element_type=jnp.float32) + up_bias.astype(
        jnp.float32
    )
    hidden = jax.nn.gelu(up_value, approximate=False).astype(jnp.bfloat16)
    result = (
        residual
        + jnp.dot(hidden, w_down, preferred_element_type=jnp.float32)
        + down_bias.astype(jnp.float32)
    )
    outgoing = jnp.dot(
        select, result.astype(jnp.bfloat16), preferred_element_type=jnp.float32
    ).astype(jnp.bfloat16)
    arrived = lax.all_to_all(
        outgoing.reshape(owners, capacity, model_width),
        "dp",
        split_axis=0,
        concat_axis=0,
        tiled=True,
    )
    returned = lax.all_to_all(
        cotangent.reshape(owners, capacity, model_width),
        "dp",
        split_axis=0,
        concat_axis=0,
        tiled=True,
    )
    grad_result = contract_rows(select, returned.reshape(owners * capacity, model_width))
    grad_low = grad_result.astype(jnp.bfloat16)
    grad_w_down = contract_rows(hidden, grad_low)
    grad_down_bias = jnp.sum(grad_result, axis=0)
    grad_hidden = contract_cols(grad_low, w_down)
    gelu_value, gelu_back = jax.vjp(partial(jax.nn.gelu, approximate=False), up_value)
    grad_up = gelu_back(grad_hidden)[0].astype(jnp.bfloat16)
    grad_w_up = contract_rows(normed_two, grad_up)
    grad_up_bias = jnp.sum(grad_up.astype(jnp.float32), axis=0)
    norm_value, norm_back = jax.vjp(layer_norm, residual, gain_two_f, shift_two_f)
    grad_inner, grad_gain_two, grad_shift_two = norm_back(contract_cols(grad_up, w_up))
    grad_residual = grad_result + grad_inner
    grad_branch = grad_residual.astype(jnp.bfloat16)
    grad_w_out = contract_rows(attended, grad_branch)
    grad_out_bias = jnp.sum(grad_branch.astype(jnp.float32), axis=0)
    grad_attended = contract_cols(grad_branch, w_out).astype(jnp.bfloat16)
    grad_queries, grad_keys, grad_values = attend_backward(
        queries.reshape(shaped),
        keys_low.reshape(shaped),
        values.reshape(shaped),
        valid_mask,
        logsum,
        grad_attended,
    )
    grad_projected = jnp.concatenate([grad_queries, grad_keys, grad_values], axis=1)
    grad_w_qkv = contract_rows(normed_one, grad_projected)
    grad_q_bias = jnp.sum(grad_queries.astype(jnp.float32), axis=0)
    grad_v_bias = jnp.sum(grad_values.astype(jnp.float32), axis=0)
    first_value, first_back = jax.vjp(layer_norm, tokens_float, gain_one_f, shift_one_f)
    grad_first, grad_gain_one, grad_shift_one = first_back(contract_cols(grad_projected, w_qkv))
    grad_inputs = grad_residual + grad_first
    gradients = (
        grad_gain_one,
        grad_shift_one,
        grad_w_qkv,
        grad_q_bias,
        grad_v_bias,
        grad_w_out,
        grad_out_bias,
        grad_gain_two,
        grad_shift_two,
        grad_w_up,
        grad_up_bias,
        grad_w_down,
        grad_down_bias,
    )
    return (arrived.reshape(owners * capacity, model_width), grad_inputs, gradients)


AXES = ("dp", "fsdp")


def flip_bit(block, bit, count):
    return lax.ppermute(block, AXES, [(i, i ^ bit) for i in range(count)])


def gather_rows(shard, bits, place, count):
    held = shard[None]
    done = []
    for bit in bits:
        other = flip_bit(held, bit, count)
        upper = (place & bit) != 0
        low_part = jnp.where(upper, other, held)
        high_part = jnp.where(upper, held, other)
        before = sum(1 for b in done if b > bit)
        lead = 2**before
        shape = (lead, held.shape[0] // lead) + shard.shape
        held = jnp.stack([low_part.reshape(shape), high_part.reshape(shape)], axis=1)
        held = held.reshape((-1,) + shard.shape)
        done.append(bit)
    return held.reshape((-1,) + shard.shape[1:])


def scatter_rows(full, bits, place, count):
    rows = full.shape[0] // count
    held = full.reshape((count, rows) + full.shape[1:])
    left = sorted(bits, reverse=True)
    for bit in bits:
        lead = 2 ** left.index(bit)
        pair = held.reshape((lead, 2, -1) + held.shape[1:])
        mine = ((place & bit) != 0).astype(jnp.int32)
        sent = lax.dynamic_index_in_dim(pair, 1 - mine, 1, keepdims=False)
        kept = lax.dynamic_index_in_dim(pair, mine, 1, keepdims=False)
        got = flip_bit(sent, bit, count)
        held = kept.astype(jnp.float32) + got.astype(jnp.float32)
        held = held.reshape((-1,) + held.shape[2:])
        left.remove(bit)
        if left:
            held = held.astype(jnp.bfloat16)
    return held[0]


def bit_orders(count):
    bits = [1 << k for k in range(count.bit_length() - 1)][::-1]
    tail = bits[-3:]
    front = bits[:-3]
    return front + tail, front + [tail[1], tail[0], tail[2]]


def to_columns(vectors, wide, rows):
    parts = [v.reshape(rows, 1) for v in vectors] + [wide.reshape(rows, -1)]
    packed = jnp.concatenate(parts, axis=1)
    return jnp.pad(packed, ((0, 0), (0, 128 - packed.shape[1])))


def body(
    cell_tokens,
    lengths,
    gene_ids,
    grad_gene,
    ln1_gain,
    ln1_bias,
    w_qkv,
    q_bias,
    v_bias,
    w_out,
    out_bias,
    ln2_gain,
    ln2_bias,
    w_up,
    up_bias,
    w_down,
    down_bias,
):
    micro_count = cell_tokens.shape[0]
    owners = lax.axis_size("dp")
    capacity = cell_tokens.shape[2] // owners
    gene_span = GENES // owners
    totals = None
    gene_parts = []
    token_parts = []
    count = owners * lax.axis_size("fsdp")
    place = lax.axis_index(AXES)
    order_one, order_two = bit_orders(count)
    rows = ln1_gain.shape[0]
    width = rows * count
    small = to_columns(
        (ln1_gain, ln1_bias, q_bias, v_bias, out_bias, ln2_gain, ln2_bias, down_bias),
        up_bias,
        rows,
    )
    ratio = up_bias.shape[0] // rows
    full_qk = gather_rows(w_qkv[:, : 2 * width], order_one, place, count)
    full_vo = gather_rows(
        jnp.concatenate([w_qkv[:, 2 * width :], w_out, small], axis=1), order_two, place, count
    )
    full_up = gather_rows(w_up, order_one, place, count)
    full_down = gather_rows(w_down, order_two, place, count)
    turned = full_vo[:, 2 * width :].T
    full_qkv = jnp.concatenate([full_qk, full_vo[:, :width]], axis=1)
    full_out = full_vo[:, width : 2 * width]
    gathered = (
        turned[0],
        turned[1],
        full_qkv,
        turned[2],
        turned[3],
        full_out,
        turned[4],
        turned[5],
        turned[6],
        full_up,
        full_vo[:, 2 * width + 8 : 2 * width + 8 + ratio].reshape(-1),
        full_down,
        turned[7],
    )
    for batch_index in range(micro_count):
        arrived, grad_inputs, gradients = micro_step(
            gathered,
            cell_tokens[batch_index, 0],
            lengths[batch_index, 0],
            gene_ids[batch_index, 0],
            grad_gene[batch_index, 0],
            owners,
            capacity,
            gene_span,
        )
        gene_parts.append(arrived)
        token_parts.append(grad_inputs)
        if totals is None:
            totals = gradients
        else:
            totals = jax.tree.map(jnp.add, totals, gradients)
    low = jnp.bfloat16
    back_one, back_two = order_one[::-1], order_two[::-1]
    sum_down = scatter_rows(totals[11].astype(low), back_two, place, count)
    sum_up = scatter_rows(totals[9].astype(low), back_one, place, count)
    small = to_columns(
        (totals[0], totals[1], totals[3], totals[4], totals[6], totals[7], totals[8], totals[12]),
        totals[10],
        width,
    )
    sum_vo = scatter_rows(
        jnp.concatenate([totals[2][:, 2 * width :], totals[5], small], axis=1).astype(low),
        back_two,
        place,
        count,
    )
    sum_qk = scatter_rows(totals[2][:, : 2 * width].astype(low), back_one, place, count)
    flat = sum_vo[:, 2 * width :].T
    totals = (
        flat[0],
        flat[1],
        jnp.concatenate([sum_qk, sum_vo[:, :width]], axis=1),
        flat[2],
        flat[3],
        sum_vo[:, width : 2 * width],
        flat[4],
        flat[5],
        flat[6],
        sum_up,
        sum_vo[:, 2 * width + 8 : 2 * width + 8 + ratio].reshape(-1),
        sum_down,
        flat[7],
    )
    gene_rows = jnp.stack(gene_parts)[:, None]
    grad_tokens = jnp.stack(token_parts)[:, None]
    return (
        gene_rows,
        grad_tokens,
        totals[0],
        totals[1],
        totals[2],
        totals[3],
        totals[4],
        totals[5],
        totals[6],
        totals[7],
        totals[8],
        totals[9],
        totals[10],
        totals[11],
        totals[12],
    )


def solution(mesh):
    placed = (
        P(None, ("dp", "fsdp"), None, None),
        P(None, ("dp", "fsdp")),
        P(None, ("dp", "fsdp"), None),
        P(None, ("dp", "fsdp"), None, None),
        P(("dp", "fsdp")),
        P(("dp", "fsdp")),
        P(("dp", "fsdp"), None),
        P(("dp", "fsdp")),
        P(("dp", "fsdp")),
        P(("dp", "fsdp"), None),
        P(("dp", "fsdp")),
        P(("dp", "fsdp")),
        P(("dp", "fsdp")),
        P(("dp", "fsdp"), None),
        P(("dp", "fsdp")),
        P(("dp", "fsdp"), None),
        P(("dp", "fsdp")),
    )
    return jax.shard_map(
        body,
        mesh=mesh,
        in_specs=placed,
        out_specs=(
            P(None, ("dp", "fsdp"), None, None),
            P(None, ("dp", "fsdp"), None, None),
            P(("dp", "fsdp")),
            P(("dp", "fsdp")),
            P(("dp", "fsdp"), None),
            P(("dp", "fsdp")),
            P(("dp", "fsdp")),
            P(("dp", "fsdp"), None),
            P(("dp", "fsdp")),
            P(("dp", "fsdp")),
            P(("dp", "fsdp")),
            P(("dp", "fsdp"), None),
            P(("dp", "fsdp")),
            P(("dp", "fsdp"), None),
            P(("dp", "fsdp")),
        ),
        check_vma=False,
    )
```

```python
from functools import partial

import jax
import jax.numpy as jnp
from jax import lax
from jax.experimental import pallas as pl
from jax.experimental.pallas import tpu as pltpu
from jax.sharding import PartitionSpec as P

GENES = 19264
HD = 64
LANES = 128
VECTORS = 16
AXES = ("dp", "fsdp")
LOW = jnp.bfloat16
FULL = jnp.float32
LN1_GAIN, LN1_BIAS, Q_BIAS, V_BIAS, OUT_BIAS, LN2_GAIN, LN2_BIAS, DOWN_BIAS = range(8)


def mat(a, b):
    return lax.dot_general(a, b, (((1,), (0,)), ((), ())), preferred_element_type=FULL)


def mat_nt(a, b):
    return lax.dot_general(a, b, (((1,), (1,)), ((), ())), preferred_element_type=FULL)


def mat_tn(a, b):
    return lax.dot_general(a, b, (((0,), (0,)), ((), ())), preferred_element_type=FULL)


def normalize(v):
    center = v - jnp.mean(v, axis=-1, keepdims=True)
    scale = lax.rsqrt(jnp.mean(center * center, axis=-1, keepdims=True) + 1e-5)
    return center * scale, scale


def normalize_back(hat, scale, grad_hat):
    mean_grad = jnp.mean(grad_hat, axis=-1, keepdims=True)
    mean_both = jnp.mean(grad_hat * hat, axis=-1, keepdims=True)
    return scale * (grad_hat - mean_grad - hat * mean_both)


def row(vec_ref, which):
    return vec_ref[which : which + 1, :]


def column_sum(v):
    return jnp.sum(v, axis=0, keepdims=True)


def head_masks():
    lane = lax.broadcasted_iota(jnp.int32, (1, LANES), 1)
    first = lane < HD
    return first, jnp.logical_not(first)


def pick(mask, v):
    return jnp.where(mask, v, jnp.zeros_like(v))


def attend_kernel(len_ref, x_ref, wqk_ref, wvo_ref, vec_ref, qkv_ref, p_ref, o_ref, r1_ref, h1_ref):
    cells, length = p_ref.shape[0], p_ref.shape[2]
    width = x_ref.shape[1]
    x = x_ref[...].astype(FULL)
    hat, _ = normalize(x)
    h1 = (hat * row(vec_ref, LN1_GAIN) + row(vec_ref, LN1_BIAS)).astype(LOW)
    h1_ref[...] = h1
    qkv_ref[:, :width] = (mat(h1, wqk_ref[:, :width]) + row(vec_ref, Q_BIAS)).astype(LOW)
    qkv_ref[:, width : 2 * width] = mat(h1, wqk_ref[:, width:]).astype(LOW)
    qkv_ref[:, 2 * width :] = (mat(h1, wvo_ref[:, :width]) + row(vec_ref, V_BIAS)).astype(LOW)
    masks = head_masks()
    key_at = lax.broadcasted_iota(jnp.int32, (length, length), 1)

    def one_pair(pair, carry):
        at = pl.multiple_of(pair * LANES, LANES)
        for cell in range(cells):
            rows = slice(cell * length, (cell + 1) * length)
            q = qkv_ref[rows, pl.ds(at, LANES)]
            k = qkv_ref[rows, pl.ds(pl.multiple_of(at + width, LANES), LANES)]
            v = qkv_ref[rows, pl.ds(pl.multiple_of(at + 2 * width, LANES), LANES)]
            seen = key_at < len_ref[cell]
            out = jnp.zeros((length, LANES), FULL)
            for half in range(2):
                s = mat_nt(pick(masks[half], q), k) * 0.125
                s = jnp.where(seen, s, -1e30)
                e = jnp.exp(s - jnp.max(s, axis=-1, keepdims=True))
                a = (e / jnp.sum(e, axis=-1, keepdims=True)).astype(LOW)
                p_ref[cell, 2 * pair + half] = a
                out = out + mat(a, pick(masks[half], v))
            o_ref[rows, pl.ds(at, LANES)] = out.astype(LOW)
        return carry

    lax.fori_loop(0, width // LANES, one_pair, 0)
    r1_ref[...] = x + mat(o_ref[...], wvo_ref[:, width : 2 * width]) + row(vec_ref, OUT_BIAS)


def gelu_pair(u):
    half = 0.5 + 0.5 * lax.erf(u * 0.7071067811865476)
    return u * half, half + u * (0.3989422804014327 * jnp.exp(-0.5 * u * u))


def slot_matrix(gene_ref, len_ref, cell, owners, span, length):
    lanes = max(LANES, owners)
    capacity = length // owners
    gene = gene_ref[cell]
    token = lax.broadcasted_iota(jnp.int32, (length, 1), 0)
    valid = token < len_ref[cell]
    start = lax.broadcasted_iota(jnp.int32, (1, lanes), 1) * span
    hits = (gene >= start) & (gene < start + span) & valid
    hits_low = hits.astype(FULL).astype(LOW)
    earlier = (
        lax.broadcasted_iota(jnp.int32, (length, length), 1)
        < lax.broadcasted_iota(jnp.int32, (length, length), 0)
    )
    counts = mat(earlier.astype(FULL).astype(LOW), hits_low)
    base = (lax.broadcasted_iota(jnp.int32, (1, lanes), 1) * capacity).astype(FULL)
    slot = jnp.sum(jnp.where(hits, counts + base, 0.0), axis=-1, keepdims=True)
    slot = jnp.where(valid, slot, -1.0)
    at = lax.broadcasted_iota(jnp.int32, (length, length), 1).astype(FULL)
    return (slot == at).astype(FULL).astype(LOW)


def feed_kernel(
    len_ref, gene_ref, ret_ref, r1_ref, vec_ref, upb_ref, wup_ref, wdown_ref,
    gup_ref, gdown_ref, gupb_ref, out_ref, g1_ref, gvec_ref,
    h2_s, h2t_s, gy_s, sel_s, y_s, dh_s, *, owners, span,
):
    step = pl.program_id(0)
    cells, length = sel_s.shape[0], sel_s.shape[1]
    width = r1_ref.shape[1]
    groups = ret_ref.shape[0]

    @pl.when(step == 0)
    def _():
        hat, _ = normalize(r1_ref[...])
        h2 = (hat * row(vec_ref, LN2_GAIN) + row(vec_ref, LN2_BIAS)).astype(LOW)
        h2_s[...] = h2
        h2t_s[...] = h2.T
        for cell in range(cells):
            sel = slot_matrix(gene_ref, len_ref, cell, owners, span, length)
            sel_s[cell] = sel
            came = ret_ref[:, cell].reshape(length, width)
            gy_s[cell * length : (cell + 1) * length, :] = mat(sel, came).astype(LOW)
        y_s[...] = r1_ref[...] + row(vec_ref, DOWN_BIAS)
        dh_s[...] = jnp.zeros_like(dh_s)

    h2 = h2_s[...]
    gy = gy_s[...]
    u = mat(h2, wup_ref[...]) + upb_ref[...]
    act, slope = gelu_pair(u)
    hm = act.astype(LOW)
    du = mat_nt(gy, wdown_ref[...]) * slope
    du_low = du.astype(LOW)
    y_s[...] += mat(hm, wdown_ref[...])
    gdown_ref[...] = mat_tn(hm, gy).astype(LOW)
    gup_ref[...] = mat(h2t_s[...], du_low).astype(LOW)
    gupb_ref[...] = column_sum(du_low.astype(FULL))
    dh_s[...] += mat_nt(du_low, wup_ref[...])

    @pl.when(step == pl.num_programs(0) - 1)
    def _():
        y = y_s[...].astype(LOW)
        for cell in range(cells):
            sent = mat_tn(sel_s[cell], y[cell * length : (cell + 1) * length, :])
            out_ref[:, cell] = sent.astype(LOW).reshape(groups, length // groups, width)
        hat, scale = normalize(r1_ref[...])
        dh = dh_s[...]
        gy_full = gy_s[...].astype(FULL)
        g1 = gy_full + normalize_back(hat, scale, dh * row(vec_ref, LN2_GAIN))
        g1_ref[...] = g1
        gvec_ref[...] = jnp.zeros_like(gvec_ref)
        gvec_ref[DOWN_BIAS : DOWN_BIAS + 1, :] = column_sum(gy_full)
        gvec_ref[LN2_GAIN : LN2_GAIN + 1, :] = column_sum(dh * hat)
        gvec_ref[LN2_BIAS : LN2_BIAS + 1, :] = column_sum(dh)
        gvec_ref[OUT_BIAS : OUT_BIAS + 1, :] = column_sum(g1.astype(LOW).astype(FULL))


def attend_back_kernel(
    x_ref, h1_ref, g1_ref, o_ref, qkv_ref, p_ref, wqk_ref, wvo_ref, vec_ref, gvec_in_ref, wide_ref,
    gx_ref, gqk_ref, gvo_ref, go_s, d_s, gvec_s,
):
    cells, length = p_ref.shape[0], p_ref.shape[2]
    width = x_ref.shape[1]
    ga = g1_ref[...].astype(LOW)
    gvo_ref[:, width : 2 * width] = mat_tn(o_ref[...], ga).astype(LOW)
    go_s[...] = mat_nt(ga, wvo_ref[:, width : 2 * width]).astype(LOW)
    masks = head_masks()

    def one_pair(pair, carry):
        at = pl.multiple_of(pair * LANES, LANES)
        at_k = pl.multiple_of(at + width, LANES)
        at_v = pl.multiple_of(at + 2 * width, LANES)
        for cell in range(cells):
            rows = slice(cell * length, (cell + 1) * length)
            q = qkv_ref[rows, pl.ds(at, LANES)]
            k = qkv_ref[rows, pl.ds(at_k, LANES)]
            v = qkv_ref[rows, pl.ds(at_v, LANES)]
            go = go_s[rows, pl.ds(at, LANES)]
            dq = jnp.zeros((length, LANES), FULL)
            dk, dv = dq, dq
            for half in range(2):
                a = p_ref[cell, 2 * pair + half]
                go_half = pick(masks[half], go)
                a_full = a.astype(FULL)
                weighted = a_full * mat_nt(go_half, v)
                ds = (weighted - a_full * jnp.sum(weighted, axis=-1, keepdims=True)).astype(LOW)
                dq = dq + mat(ds, pick(masks[half], k))
                dk = dk + mat_tn(ds, pick(masks[half], q))
                dv = dv + mat_tn(a, go_half)
            d_s[rows, pl.ds(at, LANES)] = (dq * 0.125).astype(LOW)
            d_s[rows, pl.ds(at_k, LANES)] = (dk * 0.125).astype(LOW)
            d_s[rows, pl.ds(at_v, LANES)] = dv.astype(LOW)
        return carry

    lax.fori_loop(0, width // LANES, one_pair, 0)
    h1t = h1_ref[...].T
    gqk_ref[...] = mat(h1t, d_s[:, : 2 * width]).astype(LOW)
    gvo_ref[:, :width] = mat(h1t, d_s[:, 2 * width :]).astype(LOW)
    dh = mat_nt(d_s[:, : 2 * width], wqk_ref[...]) + mat_nt(d_s[:, 2 * width :], wvo_ref[:, :width])
    hat, scale = normalize(x_ref[...].astype(FULL))
    gx_ref[...] = g1_ref[...] + normalize_back(hat, scale, dh * row(vec_ref, LN1_GAIN))
    gvec_s[:VECTORS, :] = gvec_in_ref[...]
    gvec_s[VECTORS:, :] = jnp.zeros((LANES - VECTORS, width), FULL)
    gvec_s[LN1_GAIN : LN1_GAIN + 1, :] = column_sum(dh * hat)
    gvec_s[LN1_BIAS : LN1_BIAS + 1, :] = column_sum(dh)
    gvec_s[Q_BIAS : Q_BIAS + 1, :] = column_sum(d_s[:, :width].astype(FULL))
    gvec_s[V_BIAS : V_BIAS + 1, :] = column_sum(d_s[:, 2 * width :].astype(FULL))
    gvo_ref[:, 2 * width :] = (gvec_s[...].T + wide_ref[...]).astype(LOW)


SMEM = pl.BlockSpec(memory_space=pltpu.SMEM)
VMEM = pl.BlockSpec(memory_space=pltpu.VMEM)


def attend(lengths, x, wqk, wvo, vec, cells):
    tokens, width = x.shape
    length = tokens // cells
    heads = width // HD
    shape = jax.ShapeDtypeStruct
    return pl.pallas_call(
        attend_kernel,
        out_shape=(
            shape((tokens, 3 * width), LOW),
            shape((cells, heads, length, length), LOW),
            shape((tokens, width), LOW),
            shape((tokens, width), FULL),
            shape((tokens, width), LOW),
        ),
        in_specs=[SMEM] + [VMEM] * 4,
        out_specs=(VMEM,) * 5,
        name="attend",
    )(lengths, x, wqk, wvo, vec)


def feed(lengths, genes, returned, r1, vec, up_bias, w_up, w_down, cells, owners, span):
    tokens, width = r1.shape
    length = tokens // cells
    hidden = w_up.shape[1]
    block = min(hidden, 512)
    shape = jax.ShapeDtypeStruct

    def whole(array_shape):
        return pl.BlockSpec(array_shape, lambda i: (0,) * len(array_shape))

    return pl.pallas_call(
        partial(feed_kernel, owners=owners, span=span),
        grid=(hidden // block,),
        out_shape=(
            shape((width, hidden), LOW),
            shape((hidden, width), LOW),
            shape((1, hidden), FULL),
            shape(returned.shape, LOW),
            shape((tokens, width), FULL),
            shape(vec.shape, FULL),
        ),
        in_specs=[
            SMEM,
            whole(genes.shape),
            whole(returned.shape),
            whole(r1.shape),
            whole(vec.shape),
            pl.BlockSpec((1, block), lambda i: (0, i)),
            pl.BlockSpec((width, block), lambda i: (0, i)),
            pl.BlockSpec((block, width), lambda i: (i, 0)),
        ],
        out_specs=(
            pl.BlockSpec((width, block), lambda i: (0, i)),
            pl.BlockSpec((block, width), lambda i: (i, 0)),
            pl.BlockSpec((1, block), lambda i: (0, i)),
            whole(returned.shape),
            whole(r1.shape),
            whole(vec.shape),
        ),
        scratch_shapes=[
            pltpu.VMEM((tokens, width), LOW),
            pltpu.VMEM((width, tokens), LOW),
            pltpu.VMEM((tokens, width), LOW),
            pltpu.VMEM((cells, length, length), LOW),
            pltpu.VMEM((tokens, width), FULL),
            pltpu.VMEM((tokens, width), FULL),
        ],
        name="feed",
    )(lengths, genes, returned, r1, vec, up_bias, w_up, w_down)


def attend_back(x, h1, g1, o, qkv, p, wqk, wvo, vec, gvec, wide):
    tokens, width = x.shape
    shape = jax.ShapeDtypeStruct
    return pl.pallas_call(
        attend_back_kernel,
        out_shape=(
            shape((tokens, width), FULL),
            shape((width, 2 * width), LOW),
            shape((width, 2 * width + LANES), LOW),
        ),
        in_specs=[VMEM] * 11,
        out_specs=(VMEM,) * 3,
        scratch_shapes=[
            pltpu.VMEM((tokens, width), LOW),
            pltpu.VMEM((tokens, 3 * width), LOW),
            pltpu.VMEM((LANES, width), FULL),
        ],
        name="attend_back",
    )(x, h1, g1, o, qkv, p, wqk, wvo, vec, gvec, wide)


def flip_bit(block, bit, count):
    return lax.ppermute(block, AXES, [(i, i ^ bit) for i in range(count)])


def gather_rows(shard, bits, place, count):
    held = shard[None]
    done = []
    for bit in bits:
        other = flip_bit(held, bit, count)
        upper = (place & bit) != 0
        low_part = jnp.where(upper, other, held)
        high_part = jnp.where(upper, held, other)
        before = sum(1 for b in done if b > bit)
        lead = 2**before
        shape = (lead, held.shape[0] // lead) + shard.shape
        held = jnp.stack([low_part.reshape(shape), high_part.reshape(shape)], axis=1)
        held = held.reshape((-1,) + shard.shape)
        done.append(bit)
    return held.reshape((-1,) + shard.shape[1:])


def scatter_rows(full, bits, place, count):
    rows = full.shape[0] // count
    held = full.reshape((count, rows) + full.shape[1:])
    left = sorted(bits, reverse=True)
    for bit in bits:
        lead = 2 ** left.index(bit)
        pair = held.reshape((lead, 2, -1) + held.shape[1:])
        mine = ((place & bit) != 0).astype(jnp.int32)
        sent = lax.dynamic_index_in_dim(pair, 1 - mine, 1, keepdims=False)
        kept = lax.dynamic_index_in_dim(pair, mine, 1, keepdims=False)
        got = flip_bit(sent, bit, count)
        held = kept.astype(FULL) + got.astype(FULL)
        held = held.reshape((-1,) + held.shape[2:])
        left.remove(bit)
        if left:
            held = held.astype(LOW)
    return held[0]


def bit_orders(count):
    bits = [1 << k for k in range(count.bit_length() - 1)][::-1]
    tail = bits[-3:]
    front = bits[:-3]
    return front + tail, front + [tail[1], tail[0], tail[2]]


def to_slots(rows, owners):
    cells, slots, width = rows.shape
    return rows.reshape(cells, owners, slots // owners, width).transpose(1, 0, 2, 3)


def from_slots(rows):
    owners, cells, capacity, width = rows.shape
    return rows.transpose(1, 0, 2, 3).reshape(cells, owners * capacity, width)


def swap_owners(rows):
    return lax.all_to_all(rows, "dp", split_axis=0, concat_axis=0, tiled=True)


def body(
    cell_tokens, lengths, gene_ids, grad_gene, ln1_gain, ln1_bias, w_qkv, q_bias, v_bias, w_out,
    out_bias, ln2_gain, ln2_bias, w_up, up_bias, w_down, down_bias,
):
    cells, _, length, width = cell_tokens.shape
    owners = lax.axis_size("dp")
    span = GENES // owners
    count = owners * lax.axis_size("fsdp")
    place = lax.axis_index(AXES)
    order_one, order_two = bit_orders(count)
    rows = width // count
    ratio = up_bias.shape[0] // rows
    x = cell_tokens.reshape(cells * length, width)
    seen = lengths[:, 0]
    genes = gene_ids.reshape(cells, length, 1)

    vectors = (ln1_gain, ln1_bias, q_bias, v_bias, out_bias, ln2_gain, ln2_bias, down_bias)
    small = jnp.concatenate([v[:, None] for v in vectors] + [up_bias.reshape(rows, ratio)], axis=1)
    small = jnp.pad(small, ((0, 0), (0, LANES - small.shape[1])))
    wqk = gather_rows(w_qkv[:, : 2 * width], order_one, place, count)
    wvo = gather_rows(
        jnp.concatenate([w_qkv[:, 2 * width :], w_out, small], axis=1), order_two, place, count
    )
    wup = gather_rows(w_up, order_one, place, count)
    wdown = gather_rows(w_down, order_two, place, count)
    small = wvo[:, 2 * width :]
    vec = small[:, :VECTORS].T.astype(FULL)
    wide_at = len(vectors)
    up_row = small[:, wide_at : wide_at + ratio].reshape(1, -1).astype(FULL)

    qkv, p, o, r1, h1 = attend(seen, x, wqk, wvo, vec, cells)
    returned = swap_owners(to_slots(grad_gene[:, 0], owners))
    direct = (length // owners) % 16 == 0
    if not direct:
        returned = from_slots(returned)[None]
    gup, gdown, gup_row, sent, g1, gvec = feed(
        seen, genes, returned, r1, vec, up_row, wup, wdown, cells, owners, span
    )
    if not direct:
        sent = to_slots(sent[0], owners)
    gene_rows = from_slots(swap_owners(sent))[:, None]
    wide = jnp.pad(gup_row.reshape(width, ratio), ((0, 0), (wide_at, LANES - wide_at - ratio)))
    gx, gqk, gvo = attend_back(x, h1, g1, o, qkv, p, wqk, wvo, vec, gvec, wide)

    back_one, back_two = order_one[::-1], order_two[::-1]
    sum_down = scatter_rows(gdown, back_two, place, count)
    sum_up = scatter_rows(gup, back_one, place, count)
    sum_vo = scatter_rows(gvo, back_two, place, count)
    sum_qk = scatter_rows(gqk, back_one, place, count)
    flat = sum_vo[:, 2 * width :].T
    sum_up_bias = sum_vo[:, 2 * width + wide_at : 2 * width + wide_at + ratio].reshape(-1)
    return (
        gene_rows,
        gx.reshape(cells, 1, length, width),
        flat[0],
        flat[1],
        jnp.concatenate([sum_qk, sum_vo[:, :width]], axis=1),
        flat[2],
        flat[3],
        sum_vo[:, width : 2 * width],
        flat[4],
        flat[5],
        flat[6],
        sum_up,
        sum_up_bias,
        sum_down,
        flat[7],
    )


def solution(mesh):
    placed = (
        P(None, ("dp", "fsdp"), None, None),
        P(None, ("dp", "fsdp")),
        P(None, ("dp", "fsdp"), None),
        P(None, ("dp", "fsdp"), None, None),
        P(("dp", "fsdp")),
        P(("dp", "fsdp")),
        P(("dp", "fsdp"), None),
        P(("dp", "fsdp")),
        P(("dp", "fsdp")),
        P(("dp", "fsdp"), None),
        P(("dp", "fsdp")),
        P(("dp", "fsdp")),
        P(("dp", "fsdp")),
        P(("dp", "fsdp"), None),
        P(("dp", "fsdp")),
        P(("dp", "fsdp"), None),
        P(("dp", "fsdp")),
    )
    return jax.shard_map(
        body,
        mesh=mesh,
        in_specs=placed,
        out_specs=(
            P(None, ("dp", "fsdp"), None, None),
            P(None, ("dp", "fsdp"), None, None),
            P(("dp", "fsdp")),
            P(("dp", "fsdp")),
            P(("dp", "fsdp"), None),
            P(("dp", "fsdp")),
            P(("dp", "fsdp")),
            P(("dp", "fsdp"), None),
            P(("dp", "fsdp")),
            P(("dp", "fsdp")),
            P(("dp", "fsdp")),
            P(("dp", "fsdp"), None),
            P(("dp", "fsdp")),
            P(("dp", "fsdp"), None),
            P(("dp", "fsdp")),
        ),
        check_vma=False,
    )
```

```python
from functools import partial

import jax
import jax.numpy as jnp
from jax import lax
from jax.experimental import pallas as pl
from jax.experimental.pallas import tpu as pltpu
from jax.sharding import PartitionSpec as P

GENES = 19264
HD = 64
LANES = 128
VECTORS = 16
AXES = ("dp", "fsdp")
LOW = jnp.bfloat16
FULL = jnp.float32
LN1_GAIN, LN1_BIAS, Q_BIAS, V_BIAS, OUT_BIAS, LN2_GAIN, LN2_BIAS, DOWN_BIAS = range(8)


def mat(a, b):
    return lax.dot_general(a, b, (((1,), (0,)), ((), ())), preferred_element_type=FULL)


def mat_nt(a, b):
    return lax.dot_general(a, b, (((1,), (1,)), ((), ())), preferred_element_type=FULL)


def mat_tn(a, b):
    return lax.dot_general(a, b, (((0,), (0,)), ((), ())), preferred_element_type=FULL)


def normalize(v):
    center = v - jnp.mean(v, axis=-1, keepdims=True)
    scale = lax.rsqrt(jnp.mean(center * center, axis=-1, keepdims=True) + 1e-5)
    return center * scale, scale


def normalize_back(hat, scale, grad_hat):
    mean_grad = jnp.mean(grad_hat, axis=-1, keepdims=True)
    mean_both = jnp.mean(grad_hat * hat, axis=-1, keepdims=True)
    return scale * (grad_hat - mean_grad - hat * mean_both)


def row(vec_ref, which):
    return vec_ref[which : which + 1, :]


def column_sum(v):
    return jnp.sum(v, axis=0, keepdims=True)


def head_masks():
    lane = lax.broadcasted_iota(jnp.int32, (1, LANES), 1)
    first = lane < HD
    return first, jnp.logical_not(first)


def pick(mask, v):
    return jnp.where(mask, v, jnp.zeros_like(v))


def attend_kernel(len_ref, x_ref, wqk_ref, wvo_ref, vec_ref, qkv_ref, p_ref, o_ref, r1_ref, h1_ref):
    cells, length = p_ref.shape[0], p_ref.shape[2]
    width = x_ref.shape[1]
    x = x_ref[...].astype(FULL)
    hat, _ = normalize(x)
    h1 = (hat * row(vec_ref, LN1_GAIN) + row(vec_ref, LN1_BIAS)).astype(LOW)
    h1_ref[...] = h1
    qkv_ref[:, :width] = (mat(h1, wqk_ref[:, :width]) + row(vec_ref, Q_BIAS)).astype(LOW)
    qkv_ref[:, width : 2 * width] = mat(h1, wqk_ref[:, width:]).astype(LOW)
    qkv_ref[:, 2 * width :] = (mat(h1, wvo_ref[:, :width]) + row(vec_ref, V_BIAS)).astype(LOW)
    masks = head_masks()
    key_at = lax.broadcasted_iota(jnp.int32, (length, length), 1)

    def one_pair(pair, carry):
        at = pl.multiple_of(pair * LANES, LANES)
        for cell in range(cells):
            rows = slice(cell * length, (cell + 1) * length)
            q = qkv_ref[rows, pl.ds(at, LANES)]
            k = qkv_ref[rows, pl.ds(pl.multiple_of(at + width, LANES), LANES)]
            v = qkv_ref[rows, pl.ds(pl.multiple_of(at + 2 * width, LANES), LANES)]
            seen = key_at < len_ref[cell]
            out = jnp.zeros((length, LANES), FULL)
            for half in range(2):
                s = mat_nt(pick(masks[half], q), k) * 0.125
                s = jnp.where(seen, s, -1e30)
                e = jnp.exp(s - jnp.max(s, axis=-1, keepdims=True))
                a = (e / jnp.sum(e, axis=-1, keepdims=True)).astype(LOW)
                p_ref[cell, 2 * pair + half] = a
                out = out + mat(a, pick(masks[half], v))
            o_ref[rows, pl.ds(at, LANES)] = out.astype(LOW)
        return carry

    lax.fori_loop(0, width // LANES, one_pair, 0)
    r1_ref[...] = x + mat(o_ref[...], wvo_ref[:, width : 2 * width]) + row(vec_ref, OUT_BIAS)


def gelu_pair(u):
    half = 0.5 + 0.5 * lax.erf(u * 0.7071067811865476)
    return u * half, half + u * (0.3989422804014327 * jnp.exp(-0.5 * u * u))


def slot_matrix(gene_ref, len_ref, cell, owners, span, length):
    lanes = max(LANES, owners)
    capacity = length // owners
    gene = gene_ref[cell]
    token = lax.broadcasted_iota(jnp.int32, (length, 1), 0)
    valid = token < len_ref[cell]
    start = lax.broadcasted_iota(jnp.int32, (1, lanes), 1) * span
    hits = (gene >= start) & (gene < start + span) & valid
    hits_low = hits.astype(FULL).astype(LOW)
    earlier = (
        lax.broadcasted_iota(jnp.int32, (length, length), 1)
        < lax.broadcasted_iota(jnp.int32, (length, length), 0)
    )
    counts = mat(earlier.astype(FULL).astype(LOW), hits_low)
    base = (lax.broadcasted_iota(jnp.int32, (1, lanes), 1) * capacity).astype(FULL)
    slot = jnp.sum(jnp.where(hits, counts + base, 0.0), axis=-1, keepdims=True)
    slot = jnp.where(valid, slot, -1.0)
    at = lax.broadcasted_iota(jnp.int32, (length, length), 1).astype(FULL)
    return (slot == at).astype(FULL).astype(LOW)


def open_kernel(
    len_ref, gene_ref, ret_ref, r1_ref, vec_ref, upb_ref, up_a_ref, up_b_ref,
    hm_ref, slope_ref, h2t_ref, gy_ref, sel_ref, gdown_a_ref, gdown_b_ref, h2_s, *, owners, span,
):
    cells, length = sel_ref.shape[0], sel_ref.shape[1]
    width = r1_ref.shape[1]
    side = gdown_a_ref.shape[1]
    half = up_a_ref.shape[1]
    hat, _ = normalize(r1_ref[...])
    h2 = (hat * row(vec_ref, LN2_GAIN) + row(vec_ref, LN2_BIAS)).astype(LOW)
    h2_s[...] = h2
    h2t_ref[...] = h2.T
    for cell in range(cells):
        sel = slot_matrix(gene_ref, len_ref, cell, owners, span, length)
        sel_ref[cell] = sel
        came = ret_ref[:, cell].reshape(length, width)
        gy_ref[cell * length : (cell + 1) * length, :] = mat(sel, came).astype(LOW)
    block = min(half, 512)

    for which, up_ref in enumerate((up_a_ref, up_b_ref)):

        def one_block(i, carry, which=which, up_ref=up_ref):
            at = pl.multiple_of(i * block, block)
            to = pl.multiple_of(i * block + which * half, block)
            u = mat(h2_s[...], up_ref[:, pl.ds(at, block)]) + upb_ref[:, pl.ds(to, block)]
            act, slope = gelu_pair(u)
            hm = act.astype(LOW)
            hm_ref[:, pl.ds(to, block)] = hm
            slope_ref[:, pl.ds(to, block)] = slope
            grad = mat_tn(hm, gy_ref[...]).astype(LOW)
            gdown_a_ref[pl.ds(to, block), :] = grad[:, :side]
            gdown_b_ref[pl.ds(to, block), :] = grad[:, side:]
            return carry

        lax.fori_loop(0, half // block, one_block, 0)


def close_kernel(
    r1_ref, vec_ref, hm_ref, slope_ref, h2t_ref, gy_ref, sel_ref, up_a_ref, up_b_ref,
    down_a_ref, down_b_ref,
    gup_a_ref, gup_b_ref, gupb_ref, out_ref, g1_ref, gvec_ref, y_s, dh_s,
):
    cells, length = sel_ref.shape[0], sel_ref.shape[1]
    width = r1_ref.shape[1]
    side = down_a_ref.shape[1]
    half = up_a_ref.shape[1]
    groups = out_ref.shape[0]
    block = min(half, 512)
    y_s[...] = r1_ref[...] + row(vec_ref, DOWN_BIAS)
    dh_s[...] = jnp.zeros_like(dh_s)
    for which, (up_ref, gup_ref) in enumerate(((up_a_ref, gup_a_ref), (up_b_ref, gup_b_ref))):

        def one_block(i, carry, which=which, up_ref=up_ref, gup_ref=gup_ref):
            at = pl.multiple_of(i * block, block)
            to = pl.multiple_of(i * block + which * half, block)
            down = jnp.concatenate(
                [down_a_ref[pl.ds(to, block), :], down_b_ref[pl.ds(to, block), :]], axis=1
            )
            du = (mat_nt(gy_ref[...], down) * slope_ref[:, pl.ds(to, block)]).astype(LOW)
            y_s[...] += mat(hm_ref[:, pl.ds(to, block)], down)
            gup_ref[:, pl.ds(at, block)] = mat(h2t_ref[...], du).astype(LOW)
            gupb_ref[:, pl.ds(to, block)] = column_sum(du.astype(FULL))
            dh_s[...] += mat_nt(du, up_ref[:, pl.ds(at, block)])
            return carry

        lax.fori_loop(0, half // block, one_block, 0)
    y = y_s[...].astype(LOW)
    for cell in range(cells):
        sent = mat_tn(sel_ref[cell], y[cell * length : (cell + 1) * length, :])
        out_ref[:, cell] = sent.astype(LOW).reshape(groups, length // groups, width)
    hat, scale = normalize(r1_ref[...])
    dh = dh_s[...]
    gy_full = gy_ref[...].astype(FULL)
    g1 = gy_full + normalize_back(hat, scale, dh * row(vec_ref, LN2_GAIN))
    g1_ref[...] = g1
    gvec_ref[...] = jnp.zeros_like(gvec_ref)
    gvec_ref[DOWN_BIAS : DOWN_BIAS + 1, :] = column_sum(gy_full)
    gvec_ref[LN2_GAIN : LN2_GAIN + 1, :] = column_sum(dh * hat)
    gvec_ref[LN2_BIAS : LN2_BIAS + 1, :] = column_sum(dh)
    gvec_ref[OUT_BIAS : OUT_BIAS + 1, :] = column_sum(g1.astype(LOW).astype(FULL))


def attend_back_kernel(
    x_ref, h1_ref, g1_ref, o_ref, qkv_ref, p_ref, wqk_ref, wvo_ref, vec_ref, gvec_in_ref, wide_ref,
    gx_ref, gqk_ref, gvo_ref, go_s, d_s, gvec_s,
):
    cells, length = p_ref.shape[0], p_ref.shape[2]
    width = x_ref.shape[1]
    ga = g1_ref[...].astype(LOW)
    gvo_ref[:, width : 2 * width] = mat_tn(o_ref[...], ga).astype(LOW)
    go_s[...] = mat_nt(ga, wvo_ref[:, width : 2 * width]).astype(LOW)
    masks = head_masks()

    def one_pair(pair, carry):
        at = pl.multiple_of(pair * LANES, LANES)
        at_k = pl.multiple_of(at + width, LANES)
        at_v = pl.multiple_of(at + 2 * width, LANES)
        for cell in range(cells):
            rows = slice(cell * length, (cell + 1) * length)
            q = qkv_ref[rows, pl.ds(at, LANES)]
            k = qkv_ref[rows, pl.ds(at_k, LANES)]
            v = qkv_ref[rows, pl.ds(at_v, LANES)]
            go = go_s[rows, pl.ds(at, LANES)]
            dq = jnp.zeros((length, LANES), FULL)
            dk, dv = dq, dq
            for half in range(2):
                a = p_ref[cell, 2 * pair + half]
                go_half = pick(masks[half], go)
                a_full = a.astype(FULL)
                weighted = a_full * mat_nt(go_half, v)
                ds = (weighted - a_full * jnp.sum(weighted, axis=-1, keepdims=True)).astype(LOW)
                dq = dq + mat(ds, pick(masks[half], k))
                dk = dk + mat_tn(ds, pick(masks[half], q))
                dv = dv + mat_tn(a, go_half)
            d_s[rows, pl.ds(at, LANES)] = (dq * 0.125).astype(LOW)
            d_s[rows, pl.ds(at_k, LANES)] = (dk * 0.125).astype(LOW)
            d_s[rows, pl.ds(at_v, LANES)] = dv.astype(LOW)
        return carry

    lax.fori_loop(0, width // LANES, one_pair, 0)
    h1t = h1_ref[...].T
    gqk_ref[...] = mat(h1t, d_s[:, : 2 * width]).astype(LOW)
    gvo_ref[:, :width] = mat(h1t, d_s[:, 2 * width :]).astype(LOW)
    dh = mat_nt(d_s[:, : 2 * width], wqk_ref[...]) + mat_nt(d_s[:, 2 * width :], wvo_ref[:, :width])
    hat, scale = normalize(x_ref[...].astype(FULL))
    gx_ref[...] = g1_ref[...] + normalize_back(hat, scale, dh * row(vec_ref, LN1_GAIN))
    gvec_s[:VECTORS, :] = gvec_in_ref[...]
    gvec_s[VECTORS:, :] = jnp.zeros((LANES - VECTORS, width), FULL)
    gvec_s[LN1_GAIN : LN1_GAIN + 1, :] = column_sum(dh * hat)
    gvec_s[LN1_BIAS : LN1_BIAS + 1, :] = column_sum(dh)
    gvec_s[Q_BIAS : Q_BIAS + 1, :] = column_sum(d_s[:, :width].astype(FULL))
    gvec_s[V_BIAS : V_BIAS + 1, :] = column_sum(d_s[:, 2 * width :].astype(FULL))
    gvo_ref[:, 2 * width :] = (gvec_s[...].T + wide_ref[...]).astype(LOW)


SMEM = pl.BlockSpec(memory_space=pltpu.SMEM)
VMEM = pl.BlockSpec(memory_space=pltpu.VMEM)


def cost(flops, micros):
    return pl.CostEstimate(flops=flops, transcendentals=0, bytes_accessed=micros * 3_000_000)


def attend(lengths, x, wqk, wvo, vec, cells):
    tokens, width = x.shape
    length = tokens // cells
    heads = width // HD
    shape = jax.ShapeDtypeStruct
    return pl.pallas_call(
        attend_kernel,
        out_shape=(
            shape((tokens, 3 * width), LOW),
            shape((cells, heads, length, length), LOW),
            shape((tokens, width), LOW),
            shape((tokens, width), FULL),
            shape((tokens, width), LOW),
        ),
        in_specs=[SMEM] + [VMEM] * 4,
        out_specs=(VMEM,) * 5,
        cost_estimate=cost(2 * tokens * width * 4 * width, 14),
        name="attend",
    )(lengths, x, wqk, wvo, vec)


def open_feed(lengths, genes, returned, r1, vec, up_bias, up_a, up_b, cells, owners, span):
    tokens, width = r1.shape
    length = tokens // cells
    hidden = 2 * up_a.shape[1]
    shape = jax.ShapeDtypeStruct
    return pl.pallas_call(
        partial(open_kernel, owners=owners, span=span),
        out_shape=(
            shape((tokens, hidden), LOW),
            shape((tokens, hidden), FULL),
            shape((width, tokens), LOW),
            shape((tokens, width), LOW),
            shape((cells, length, length), LOW),
            shape((hidden, width // 2), LOW),
            shape((hidden, width // 2), LOW),
        ),
        in_specs=[SMEM] + [VMEM] * 7,
        out_specs=(VMEM,) * 7,
        scratch_shapes=[pltpu.VMEM((tokens, width), LOW)],
        cost_estimate=cost(4 * tokens * width * hidden, 12),
        name="open_feed",
    )(lengths, genes, returned, r1, vec, up_bias, up_a, up_b)


def close_feed(r1, vec, hm, slope, h2t, gy, sel, up_a, up_b, down_a, down_b, returned):
    tokens, width = r1.shape
    hidden = hm.shape[1]
    shape = jax.ShapeDtypeStruct
    return pl.pallas_call(
        close_kernel,
        out_shape=(
            shape(up_a.shape, LOW),
            shape(up_b.shape, LOW),
            shape((1, hidden), FULL),
            shape(returned.shape, LOW),
            shape((tokens, width), FULL),
            shape(vec.shape, FULL),
        ),
        in_specs=[VMEM] * 11,
        out_specs=(VMEM,) * 6,
        scratch_shapes=[pltpu.VMEM((tokens, width), FULL), pltpu.VMEM((tokens, width), FULL)],
        cost_estimate=cost(8 * tokens * width * hidden, 13),
        name="close_feed",
    )(r1, vec, hm, slope, h2t, gy, sel, up_a, up_b, down_a, down_b)


def attend_back(x, h1, g1, o, qkv, p, wqk, wvo, vec, gvec, wide):
    tokens, width = x.shape
    shape = jax.ShapeDtypeStruct
    return pl.pallas_call(
        attend_back_kernel,
        out_shape=(
            shape((tokens, width), FULL),
            shape((width, 2 * width), LOW),
            shape((width, 2 * width + LANES), LOW),
        ),
        in_specs=[VMEM] * 11,
        out_specs=(VMEM,) * 3,
        scratch_shapes=[
            pltpu.VMEM((tokens, width), LOW),
            pltpu.VMEM((tokens, 3 * width), LOW),
            pltpu.VMEM((LANES, width), FULL),
        ],
        cost_estimate=cost(4 * tokens * width * 4 * width, 20),
        name="attend_back",
    )(x, h1, g1, o, qkv, p, wqk, wvo, vec, gvec, wide)


def flip_bit(block, bit, count):
    return lax.ppermute(block, AXES, [(i, i ^ bit) for i in range(count)])


def after(value, *others):
    return lax.optimization_barrier((value,) + others)[0]


def each_block(lead, inner, step):
    def one(i, carry):
        step(i // inner, lax.rem(i, inner))
        return carry

    lax.fori_loop(0, lead * inner, one, 0)


def merge_kernel(mine_ref, *refs):
    parts = len(refs) // 3
    for part in range(parts):
        held, other, out = refs[part], refs[parts + part], refs[2 * parts + part]

        def step(i, j, held=held, other=other, out=out, mine=mine_ref[part]):
            out[i, mine, j] = held[i, j]
            out[i, 1 - mine, j] = other[i, j]

        each_block(out.shape[0], out.shape[2], step)


def split_kernel(mine_ref, *refs):
    parts = mine_ref.shape[0]
    sources, outs = refs[: -2 * parts], refs[-2 * parts :]
    for part in range(parts):
        own, came = sources[part], sources[parts + part] if len(sources) > parts else None
        sent, kept = outs[part], outs[parts + part]

        def step(i, j, own=own, came=came, sent=sent, kept=kept, mine=mine_ref[part]):
            for out, which in ((sent, 1 - mine), (kept, mine)):
                value = own[i, which, j]
                if came is not None:
                    value = (value.astype(FULL) + came[i, which, j].astype(FULL)).astype(LOW)
                out[i, j] = value

        each_block(own.shape[0], own.shape[2], step)


def bit_flags(parts, at, place):
    return jnp.stack([((place & part.bits[at]) != 0).astype(jnp.int32) for part in parts])


class Gather:
    def __init__(self, shard, bits):
        self.held, self.tail = shard[None], shard.shape
        self.bits, self.done = bits, []


def gather_step(parts, place, count, *earlier):
    at = len(parts[0].done)
    helds = [after(part.held, *earlier) if earlier else part.held for part in parts]
    others = [flip_bit(held, part.bits[at], count) for held, part in zip(helds, parts)]
    shapes, views = [], []
    for part, held, other in zip(parts, helds, others):
        lead = 2 ** sum(1 for b in part.done if b > part.bits[at])
        inner = held.shape[0] // lead
        views.append([v.reshape((lead, inner) + part.tail) for v in (held, other)])
        shapes.append(jax.ShapeDtypeStruct((lead, 2, inner) + part.tail, LOW))
    outs = pl.pallas_call(
        merge_kernel,
        out_shape=tuple(shapes),
        in_specs=[SMEM] + [VMEM] * (2 * len(parts)),
        out_specs=(VMEM,) * len(parts),
        cost_estimate=cost(0, 1),
        name="merge",
    )(bit_flags(parts, at, place), *[v[0] for v in views], *[v[1] for v in views])
    for part, out in zip(parts, outs):
        part.held = out.reshape((-1,) + part.tail)
        part.done.append(part.bits[at])
    return tuple(others)


def gathered(parts):
    return [part.held.reshape((-1,) + part.tail[1:]) for part in parts]


class Scatter:
    def __init__(self, full, bits, count):
        self.own = full.reshape((count, full.shape[0] // count) + full.shape[1:])
        self.came = None
        self.bits, self.left = bits, sorted(bits, reverse=True)


def scatter_halves(parts, place):
    at = len(parts[0].bits) - len(parts[0].left)
    views, shapes = [], []
    for part in parts:
        tail = part.own.shape[1:]
        lead = 2 ** part.left.index(part.bits[at])
        inner = part.own.shape[0] // (2 * lead)
        views.append((lead, 2, inner) + tail)
        shapes.append(jax.ShapeDtypeStruct((lead, inner) + tail, LOW))
    sources = [part.own.reshape(view) for part, view in zip(parts, views)]
    if parts[0].came is not None:
        sources += [part.came.reshape(view) for part, view in zip(parts, views)]
    outs = pl.pallas_call(
        split_kernel,
        out_shape=tuple(shapes + shapes),
        in_specs=[SMEM] + [VMEM] * len(sources),
        out_specs=(VMEM,) * (2 * len(parts)),
        cost_estimate=cost(0, 1),
        name="split",
    )(bit_flags(parts, at, place), *sources)
    for part, sent, kept in zip(parts, outs[: len(parts)], outs[len(parts) :]):
        part.own = kept.reshape((-1,) + kept.shape[2:])
        part.sent = sent.reshape(part.own.shape)
    return tuple(part.sent for part in parts)


def scatter_send(parts, count, *earlier):
    at = len(parts[0].bits) - len(parts[0].left)
    for part in parts:
        sent = after(part.sent, *earlier) if earlier else part.sent
        part.came = flip_bit(sent, part.bits[at], count)
        part.left.remove(part.bits[at])
    return tuple(part.came for part in parts)


def scattered(parts):
    return [part.own[0].astype(FULL) + part.came[0].astype(FULL) for part in parts]


def bit_orders(count):
    bits = [1 << k for k in range(count.bit_length() - 1)][::-1]
    tail = bits[-3:]
    front = bits[:-3]
    return front + tail, front + [tail[1], tail[0], tail[2]]


def to_slots(rows, owners):
    cells, slots, width = rows.shape
    return rows.reshape(cells, owners, slots // owners, width).transpose(1, 0, 2, 3)


def from_slots(rows):
    owners, cells, capacity, width = rows.shape
    return rows.transpose(1, 0, 2, 3).reshape(cells, owners * capacity, width)


def swap_owners(rows):
    return lax.all_to_all(rows, "dp", split_axis=0, concat_axis=0, tiled=True)


def body(
    cell_tokens, lengths, gene_ids, grad_gene, ln1_gain, ln1_bias, w_qkv, q_bias, v_bias, w_out,
    out_bias, ln2_gain, ln2_bias, w_up, up_bias, w_down, down_bias,
):
    cells, _, length, width = cell_tokens.shape
    owners = lax.axis_size("dp")
    span = GENES // owners
    count = owners * lax.axis_size("fsdp")
    place = lax.axis_index(AXES)
    order_one, order_two = bit_orders(count)
    rows = width // count
    ratio = up_bias.shape[0] // rows
    x = cell_tokens.reshape(cells * length, width)
    seen = lengths[:, 0]
    genes = gene_ids.reshape(cells, length, 1)

    vectors = (ln1_gain, ln1_bias, q_bias, v_bias, out_bias, ln2_gain, ln2_bias, down_bias)
    small = jnp.concatenate(vectors).reshape(len(vectors), rows).T
    small = jnp.concatenate([small, up_bias.reshape(rows, ratio)], axis=1)
    small = jnp.pad(small, ((0, 0), (0, LANES - small.shape[1])))
    half, side = w_up.shape[1] // 2, width // 2
    wvo = jnp.concatenate([w_qkv[:, 2 * width :], w_out, small], axis=1)
    first = [Gather(w_qkv[:, : 2 * width], order_one), Gather(wvo, order_two)]
    up = [Gather(w_up[:, :half], order_one), Gather(w_up[:, half:], order_two)]
    down = [Gather(w_down[:, :side], order_one), Gather(w_down[:, side:], order_two)]
    marks = ()
    early_mark = None
    for wave in range(len(order_one)):
        moved = ()
        for lag, chunk in enumerate((first, up, down)):
            if wave >= lag:
                moved += gather_step(chunk, place, count, *marks)
        marks = moved
        if wave == 1:
            early_mark = moved[0]
    wqk, wvo = gathered(first)
    small = wvo[:, 2 * width :]
    vec = small[:, :VECTORS].T.astype(FULL)
    wide_at = len(vectors)
    up_row = small[:, wide_at : wide_at + ratio].reshape(1, -1).astype(FULL)

    returned = swap_owners(after(to_slots(grad_gene[:, 0], owners), early_mark))
    direct = (length // owners) % 16 == 0
    if not direct:
        returned = from_slots(returned)[None]
    qkv, p, o, r1, h1 = attend(seen, x, wqk, wvo, vec, cells)
    gather_step(up, place, count, r1)
    gather_step(down, place, count, r1)
    up_a, up_b = gathered(up)
    hm, slope, h2t, gy, sel, gdown_a, gdown_b = open_feed(
        seen, genes, returned, r1, vec, up_row, up_a, up_b, cells, owners, span
    )
    back_one, back_two = order_one[::-1], order_two[::-1]
    sum_down = [Scatter(gdown_a, back_one, count), Scatter(gdown_b, back_two, count)]
    gather_step(down, place, count, gy)
    scatter_halves(sum_down, place)
    scatter_send(sum_down, count)
    next_sent = scatter_halves(sum_down, place)
    scatter_send(sum_down, count)
    down_a, down_b = gathered(down)
    gup_a, gup_b, gup_row, sent, g1, gvec = close_feed(
        after(r1, *next_sent), vec, hm, slope, h2t, gy, sel, up_a, up_b, down_a, down_b, returned
    )
    if not direct:
        sent = to_slots(sent[0], owners)
    arrived = swap_owners(sent)
    sum_up = [Scatter(gup_a, back_one, count), Scatter(gup_b, back_two, count)]
    scatter_halves(sum_up, place)
    scatter_send(sum_up, count)
    sum_down[0].own = after(sum_down[0].own, g1)
    scatter_halves(sum_down, place)
    scatter_send(sum_down, count)
    sent_up = scatter_halves(sum_up, place)
    sent_down = scatter_halves(sum_down, place)
    marks = scatter_send(sum_up, count) + scatter_send(sum_down, count)
    wide = jnp.pad(gup_row.reshape(width, ratio), ((0, 0), (wide_at, LANES - wide_at - ratio)))
    gx, gqk, gvo = attend_back(
        x, h1, after(g1, *sent_up, *sent_down), o, qkv, p, wqk, wvo, vec, gvec, wide
    )
    sum_first = [Scatter(gqk, back_one, count), Scatter(gvo, back_two, count)]
    for part in (sum_up[0], sum_down[0]):
        part.own = after(part.own, gx)
    waiting = [sum_first, sum_up, sum_down]
    marks = ()
    while waiting:
        for parts in waiting:
            scatter_halves(parts, place)
        moved = ()
        for parts in waiting:
            moved += scatter_send(parts, count, *marks)
        marks = moved
        waiting = [parts for parts in waiting if parts[0].left]
    (down_a, down_b), (up_a, up_b) = scattered(sum_down), scattered(sum_up)
    sum_qk, sum_vo = scattered(sum_first)
    arrived = after(arrived, *marks)
    gene_rows = from_slots(arrived)[:, None]
    flat = sum_vo[:, 2 * width :].T
    sum_up_bias = sum_vo[:, 2 * width + wide_at : 2 * width + wide_at + ratio].reshape(-1)
    return (
        gene_rows,
        gx.reshape(cells, 1, length, width),
        flat[0],
        flat[1],
        jnp.concatenate([sum_qk, sum_vo[:, :width]], axis=1),
        flat[2],
        flat[3],
        sum_vo[:, width : 2 * width],
        flat[4],
        flat[5],
        flat[6],
        jnp.concatenate([up_a, up_b], axis=1),
        sum_up_bias,
        jnp.concatenate([down_a, down_b], axis=1),
        flat[7],
    )


def solution(mesh):
    placed = (
        P(None, ("dp", "fsdp"), None, None),
        P(None, ("dp", "fsdp")),
        P(None, ("dp", "fsdp"), None),
        P(None, ("dp", "fsdp"), None, None),
        P(("dp", "fsdp")),
        P(("dp", "fsdp")),
        P(("dp", "fsdp"), None),
        P(("dp", "fsdp")),
        P(("dp", "fsdp")),
        P(("dp", "fsdp"), None),
        P(("dp", "fsdp")),
        P(("dp", "fsdp")),
        P(("dp", "fsdp")),
        P(("dp", "fsdp"), None),
        P(("dp", "fsdp")),
        P(("dp", "fsdp"), None),
        P(("dp", "fsdp")),
    )
    return jax.shard_map(
        body,
        mesh=mesh,
        in_specs=placed,
        out_specs=(
            P(None, ("dp", "fsdp"), None, None),
            P(None, ("dp", "fsdp"), None, None),
            P(("dp", "fsdp")),
            P(("dp", "fsdp")),
            P(("dp", "fsdp"), None),
            P(("dp", "fsdp")),
            P(("dp", "fsdp")),
            P(("dp", "fsdp"), None),
            P(("dp", "fsdp")),
            P(("dp", "fsdp")),
            P(("dp", "fsdp")),
            P(("dp", "fsdp"), None),
            P(("dp", "fsdp")),
            P(("dp", "fsdp"), None),
            P(("dp", "fsdp")),
        ),
        check_vma=False,
    )
```
